256 devices in a mesh: section: 8 (over y, core), dp: 32 (over x, z).
Axes of the slice: x: 4, y: 4, z: 8, core: 2. Of those that a mesh axis runs over, the one named last changes fastest.
Arguments:
- tokens: bfloat16 [4, 1024, 2048], P(None, 'dp'), may hold values from -6 to 6
- norm_gain: bfloat16 [8, 2048], P('section'), may hold values from 0.25 to 1.75
- router_weight: bfloat16 [8, 2048, 32], P('section'), may hold values from -0.125 to 0.125
- gate_weight: bfloat16 [8, 32, 2048, 768], P('section', 'dp'), may hold values from -0.125 to 0.125
- up_weight: bfloat16 [8, 32, 2048, 768], P('section', 'dp'), may hold values from -0.125 to 0.125
- down_weight: bfloat16 [8, 32, 768, 2048], P('section', 'dp'), may hold values from -0.21875 to 0.21875
- routing: int32 [8, 4, 1024, 6], P('section', None, 'dp'), may hold values from 0 to 31, all different within a row; in each aligned block of 32 rows (0 to 31, 32 to 63, ..., all dimensions but the last counted through in order) at most 7 rows name the same one
Outputs:
- layer_outputs: bfloat16 [8, 4, 1024, 2048], P('section', None, 'dp')
- router_grad: float32 [8, 2048, 32], P('section', 'dp')
The draws below stay inside these ranges and needn't reach their ends.
Inputs may be any that keep to these rules, and one draw needn't show every extreme that they name: `routing`: each token names 6 different experts. Among one index of dp's 32 tokens of one micro-batch and layer, at most 7 name the same expert, and in some of these blocks exactly 7 do.
All inputs are finite; a program needn't handle non-finite values.
Results may differ from the reference program's by a relative error of at most 0.019.
Values may be sent and summed in bfloat16 or wider, within the bound.
A program may use at most 64 MiB of HBM per device.

```python
import math
import jax
import jax.numpy as jnp
import numpy as np
from jax import lax

D = 2048
FFE = 768
TOPK = 6
MICRO = 4
MB_TOK = 32
EXPERTS = 32
TOKENS = 1024
CAP = 7
N_SECTION = 8
N_DP = 32


def raised(values, stream_key, source, target, shards_of, factor):
    def block_of(position):
        return (jnp.arange(values.shape[position]) // (values.shape[position] // shards_of)).reshape((-1,) + (1,) * (values.ndim - 1 - position))

    first = jax.random.permutation(stream_key, shards_of)[block_of(target)]
    other_side = (block_of(target) + shards_of // 2) % shards_of
    return jnp.where((block_of(source) == first) | (block_of(source) == other_side), factor * values, values)


def block_scale(rng, dims, cuts, smallest, high):
    factor_of = 1.0
    for dim, parts in cuts:
        heights = jax.random.uniform(jax.random.fold_in(jax.random.fold_in(rng, 6), dim), (parts,), jnp.float32, smallest / len(cuts), high / len(cuts))
        factor_of = factor_of * jnp.repeat(jnp.exp(heights), dims[dim] // parts).reshape((-1,) + (1,) * (len(dims) - 1 - dim))
    return factor_of


def deal_out(rng, own, number, rows, amount, top, most, lean):
    sequence = jax.random.permutation(rng, amount)
    crowded, common = portions_of(amount, rows * top, most, lean, True), portions_of(amount, rows * top, most, lean, False)
    places = jnp.arange(amount)

    def named(lengths, offset_by):
        used = int((lengths > 0).sum())
        fixed = max(1, used // 4)
        moved = fixed + (places - fixed + offset_by * (used - fixed)) % max(1, amount - fixed)
        return jnp.zeros((amount,), jnp.int32).at[sequence[jnp.where(places < fixed, places, moved)]].set(jnp.asarray(lengths, jnp.int32))

    lengths = jnp.where(number % 4 == 0, named(crowded, number // 4), named(common, number - number // 4 - 1))
    mixed = jax.random.permutation(jax.random.fold_in(own, 3), amount)
    source_of, receiver = mixed[0:amount // 2 * 2:2], mixed[1:amount // 2 * 2:2]
    slack = jnp.minimum(lengths[source_of] - 1, most - lengths[receiver]) // 2
    slack = jnp.where((source_of == sequence[0]) | (receiver == sequence[0]) | (lengths[receiver] == 0), 0, jnp.maximum(slack, 0))
    moved = jax.random.randint(jax.random.fold_in(own, 4), (amount // 2,), 0, 1 << 20) % (slack + 1)
    lengths = lengths.at[source_of].add(-moved).at[receiver].add(moved)
    items = jnp.searchsorted(jnp.cumsum(lengths), jnp.arange(rows * top), side="right").astype(jnp.int32)
    listing = items.reshape(top, rows).T
    listing = listing[jax.random.permutation(jax.random.fold_in(own, 1), rows)]
    offset_by = jax.random.randint(jax.random.fold_in(own, 2), (rows, 1), 0, top)
    return jnp.take_along_axis(listing, (jnp.arange(top)[None, :] + offset_by) % top, axis=1)


def portions_of(count, total, reach, skew, full):
    weights = [(1 << 20) // math.isqrt(grade ** skew) + 1 for grade in range(1, count + 1)]
    largest = reach if full else min(reach, max(-(-total // count), total * weights[0] // sum(weights)))
    least = 1 if total - largest >= count - 1 else 0
    holding, rest = [largest] + [least] * (count - 1), total - largest - least * (count - 1)
    while rest > 0:
        free = [i for i in range(1, count) if holding[i] < largest] or [i for i in range(1, count) if holding[i] < reach]
        whole, budget = sum([weights[i] for i in free]), rest
        for i in free:
            more = min(reach - holding[i], max(1, budget * weights[i] // whole), rest)
            holding[i] = holding[i] + more
            rest = rest - more
    return np.array(holding)


def scatter_about(key, shape, spread, limit, pieces=(), kind=jnp.bfloat16):
    drawn = jax.random.normal(key, shape, jnp.float32) * spread
    if len(pieces) > 0:
        drawn = block_scale(key, shape, pieces, -0.22, 0.18) * drawn
    return jnp.clip(drawn, min=-limit, max=limit).astype(kind)


def heavy_noise(key, shape, scale, most, shards, heavy, kind=jnp.bfloat16):
    values = scale * jax.random.normal(key, shape, jnp.float32)
    if shards:
        values = values * block_scale(key, shape, shards, -0.22, 0.18)
    return jnp.clip(raised(values, jax.random.fold_in(key, 3), *heavy), -most, most).astype(kind)


def setup_inputs(seed: int = 0) -> dict:
    splits = jax.random.split(jax.random.key(seed), 8)
    tokens = heavy_noise(splits[0], (MICRO, TOKENS, D), 1.0, 6.0, ((1, 32),), (1, 2, 32, 2.75))
    norm_gain = jnp.clip(1.0 + 0.15 * jax.random.normal(splits[1], (N_SECTION, D), jnp.float32), 0.25, 1.75).astype(jnp.bfloat16)
    router_weight = scatter_about(splits[2], (N_SECTION, D, EXPERTS), D ** -0.5, 0.125, ((0, 8),))
    gate_weight = scatter_about(splits[3], (N_SECTION, EXPERTS, D, FFE), D ** -0.5, 0.125, ((0, 8), (1, 32)))
    up_weight = scatter_about(splits[4], (N_SECTION, EXPERTS, D, FFE), D ** -0.5, 0.125, ((0, 8), (1, 32)))
    down_weight = scatter_about(splits[5], (N_SECTION, EXPERTS, FFE, D), FFE ** -0.5, 0.21875, ((0, 8), (1, 32)))
    routing_keys = jax.random.split(jax.random.fold_in(splits[6], 1), N_SECTION * MICRO * TOKENS // MB_TOK)
    routing_turns = jax.random.permutation(jax.random.fold_in(splits[6], 3), N_SECTION * MICRO * TOKENS // MB_TOK)
    routing = jax.vmap(lambda own, number: deal_out(jax.random.fold_in(splits[6], 2), own, number, MB_TOK, EXPERTS, TOPK, CAP, 1))(routing_keys, routing_turns).reshape((N_SECTION, MICRO, TOKENS, TOPK))
    return dict(tokens=tokens, norm_gain=norm_gain, router_weight=router_weight, gate_weight=gate_weight, up_weight=up_weight, down_weight=down_weight, routing=routing)


EPSILON = 1e-06

def normalize(states, gain):
    values = states.astype(jnp.float32)
    mean_square = lax.optimization_barrier(jnp.mean(values * values, axis=-1, keepdims=True))
    return (values * lax.rsqrt(mean_square + EPSILON) * gain.astype(jnp.float32)).astype(jnp.bfloat16)

def expert_ffn(rows, w_gate, w_up, w_down):
    gated = jnp.dot(rows, w_gate, preferred_element_type=jnp.float32)
    upward = jnp.dot(rows, w_up, preferred_element_type=jnp.float32)
    hidden = (jax.nn.silu(gated) * upward).astype(jnp.bfloat16)
    return jnp.dot(hidden, w_down, preferred_element_type=jnp.float32).astype(jnp.bfloat16)

def routed_hot(routes):
    expert_ids = jnp.arange(EXPERTS, dtype=jnp.int32)
    return (routes[..., None] == expert_ids).astype(jnp.int32).sum(axis=-2)

def layer_block(states, routes, gain, w_router, w_gate, w_up, w_down):
    normed = normalize(states, gain)
    logits = jnp.dot(normed, w_router, preferred_element_type=jnp.float32)
    exps = jnp.exp(logits)
    probs = exps / lax.optimization_barrier(jnp.sum(exps, axis=-1, keepdims=True))
    hot = routed_hot(routes).reshape(N_DP, MB_TOK, EXPERTS)
    rank = jnp.cumsum(hot, axis=1) - hot
    slot_ids = jnp.arange(CAP, dtype=jnp.int32)
    match = ((hot[..., None] == 1) & (rank[..., None] == slot_ids)).astype(jnp.float32)
    blocks = normed.reshape(N_DP, MB_TOK, D).astype(jnp.float32)
    sent = jnp.einsum('jtec,jtd->ejcd', match, blocks).astype(jnp.bfloat16)
    sent = sent.reshape(EXPERTS, N_DP * CAP, D)
    produced = lax.map(lambda item: expert_ffn(item[0], item[1], item[2], item[3]), (sent, w_gate, w_up, w_down))
    produced = lax.optimization_barrier(produced).astype(jnp.float32).reshape(EXPERTS, N_DP, CAP, D)
    chosen = hot.reshape(TOKENS, EXPERTS).astype(jnp.float32) * probs
    weights = (chosen / lax.optimization_barrier(jnp.sum(chosen, axis=-1, keepdims=True))).astype(jnp.bfloat16)
    weights = lax.optimization_barrier(weights).astype(jnp.float32).reshape(N_DP, MB_TOK, EXPERTS)
    combine = match * weights[..., None]
    mixed = jnp.einsum('jtec,ejcd->jtd', combine, produced).reshape(TOKENS, D)
    result = (states.astype(jnp.float32) + mixed).astype(jnp.bfloat16)
    return (result, normed, probs)

def reference(tokens, norm_gain, router_weight, gate_weight, up_weight, down_weight, routing):
    states = tokens
    results = []
    gradients = []
    for layer in range(N_SECTION):

        def run(item):
            return layer_block(item[0], item[1], norm_gain[layer], router_weight[layer], gate_weight[layer], up_weight[layer], down_weight[layer])
        result, normed, probs = lax.map(run, (states, routing[layer]))
        counts = lax.optimization_barrier(jnp.sum(routed_hot(routing[layer]), axis=(0, 1)))
        share = EXPERTS * counts.astype(jnp.float32) / (TOPK * MICRO * TOKENS)
        slope = probs * (share - lax.optimization_barrier(jnp.sum(probs * share, axis=-1, keepdims=True)))
        flat_normed = normed.reshape(MICRO * TOKENS, D).astype(jnp.float32)
        gradient = lax.dot_general(flat_normed, slope.reshape(MICRO * TOKENS, EXPERTS), (((0,), (0,)), ((), ())), precision=lax.Precision.HIGHEST)
        results.append(result)
        gradients.append(gradient)
        states = result
    return (jnp.stack(results), jnp.stack(gradients))
```

```python
import jax
import jax.numpy as jnp
from jax import lax
from jax.sharding import Mesh
from jax.sharding import PartitionSpec as P

DP = ("dp_0", "dp_1")


EPSILON = 1e-06


def over_axes(shard, axes):
    for axis in axes:
        shard = lax.psum(shard, axis)
    return shard


def from_behind(value, axis, steps):
    count = lax.axis_size(axis)
    initial, last = (max(0, -steps), min(count, count - steps))
    return lax.ppermute(value, axis, [(source, source + steps) for source in range(initial, last)])


def cut_along(shard, dim, peers):
    shape = shard.shape
    pieces = shard.reshape(*shape[:dim], peers, shape[dim] // peers, *shape[dim + 1 :])
    return jnp.moveaxis(pieces, dim, 0)


def summed_on_arrival(shard, axis, dim):
    pieces = cut_along(shard, dim, lax.axis_size(axis))
    arrived = lax.all_to_all(pieces, axis, split_axis=0, concat_axis=0, tiled=True)
    return arrived.astype(jnp.float32).sum(axis=0)


def normalize(states, gain):
    values = states.astype(jnp.float32)
    mean_square = jnp.mean(values * values, axis=-1, keepdims=True)
    return (values * lax.rsqrt(mean_square + EPSILON) * gain.astype(jnp.float32)).astype(
        jnp.bfloat16
    )


def expert_ffn(rows, w_gate, w_up, w_down):
    gated = jnp.dot(rows, w_gate, preferred_element_type=jnp.float32)
    upward = jnp.dot(rows, w_up, preferred_element_type=jnp.float32)
    hidden = (jax.nn.silu(gated) * upward).astype(jnp.bfloat16)
    return jnp.dot(hidden, w_down, preferred_element_type=jnp.float32).astype(jnp.bfloat16)


def slope_of(probs, share):
    return probs * (share - jnp.sum(probs * share, axis=-1, keepdims=True))


def outer_rows(normed_rows, slope_rows):
    return lax.dot_general(
        normed_rows.astype(jnp.float32),
        slope_rows,
        (((0,), (0,)), ((), ())),
        precision=lax.Precision.HIGHEST,
    )


def place(stack, index, value, active):
    previous = lax.dynamic_index_in_dim(stack, index, 0, keepdims=False)
    return lax.dynamic_update_index_in_dim(stack, jnp.where(active, value, previous), index, 0)


def on_device(tokens, norm_gain, router_weight, gate_weight, up_weight, down_weight, routing):
    sections = lax.axis_size("section")
    replicas = lax.axis_size(DP)
    position = lax.axis_index("section")
    micro = tokens.shape[0]
    rows = tokens.shape[1]
    width = tokens.shape[2]
    experts = router_weight.shape[2]
    chosen_count = routing.shape[3]
    slots = min(rows, rows * chosen_count // experts + 1)
    total_rows = micro * rows * replicas
    gain = norm_gain[0]
    w_router = router_weight[0]
    w_gate = gate_weight[0, 0]
    w_up = up_weight[0, 0]
    w_down = down_weight[0, 0]
    expert_ids = jnp.arange(experts, dtype=jnp.int32)
    hot_all = (routing[0][..., None] == expert_ids).astype(jnp.int32).sum(axis=2)
    local_counts = jnp.sum(hot_all, axis=(0, 1))
    slot_ids = jnp.arange(slots, dtype=jnp.int32)
    row_ids = jnp.arange(rows, dtype=jnp.int32)
    before = (row_ids[:, None] > row_ids[None, :]).astype(jnp.bfloat16)

    def section_work(states, hot, active):
        normed = normalize(states, gain)
        logits = jnp.dot(normed, w_router, preferred_element_type=jnp.float32)
        exps = jnp.exp(logits)
        probs = exps / jnp.sum(exps, axis=-1, keepdims=True)
        rank = jnp.dot(before, hot.astype(jnp.bfloat16), preferred_element_type=jnp.float32).astype(jnp.int32)
        match = ((hot.T[:, None, :] == 1) & (rank.T[:, None, :] == slot_ids[None, :, None])).astype(
            jnp.bfloat16
        )
        sent = jnp.einsum("ect,td->ecd", match, normed, preferred_element_type=jnp.float32).astype(
            jnp.bfloat16
        )

        def compute(flat):
            return expert_ffn(flat, w_gate, w_up, w_down)

        def skipped(flat):
            return jnp.zeros((flat.shape[0], width), jnp.bfloat16)

        received = lax.all_to_all(sent, DP, split_axis=0, concat_axis=0, tiled=True)
        flat = received.reshape(-1, width)
        produced = lax.cond(active, compute, skipped, flat)
        returned = lax.all_to_all(
            produced.reshape(received.shape), DP, split_axis=0, concat_axis=0, tiled=True
        )
        chosen = hot.astype(jnp.float32) * probs
        weights = (chosen / jnp.sum(chosen, axis=-1, keepdims=True)).astype(jnp.bfloat16)
        combine = match * weights.T[:, None, :]
        mixed = jnp.einsum("ect,ecd->td", combine, returned, preferred_element_type=jnp.float32)
        result = (states.astype(jnp.float32) + mixed).astype(jnp.bfloat16)
        return (result, normed, probs)

    def advance(step, incoming):
        index = step - position
        active = (index >= 0) & (index < micro)
        clipped = jnp.clip(index, 0, micro - 1)
        first = lax.dynamic_index_in_dim(tokens, jnp.minimum(step, micro - 1), 0, keepdims=False)
        states = jnp.where(position == 0, first, incoming)
        hot = lax.dynamic_index_in_dim(hot_all, clipped, 0, keepdims=False)
        result, normed, probs = section_work(states, hot, active)
        passed = from_behind(result, "section", 1)
        return (active, clipped, result, normed, probs, passed)

    steps = micro + sections - 1
    incoming = jnp.zeros((rows, width), jnp.bfloat16)
    outputs = jnp.zeros((micro, rows, width), jnp.bfloat16)
    counts = over_axes(local_counts, DP)
    share = experts * counts.astype(jnp.float32) / (chosen_count * total_rows)

    def loop_before(step, carry):
        received, stored, gradient = carry
        active, clipped, result, normed, probs, passed = advance(step, received)
        contribution = outer_rows(normed, slope_of(probs, share))
        gradient = gradient + jnp.where(active, contribution, jnp.zeros_like(contribution))
        return (passed, place(stored, clipped, result, active), gradient)

    start_carry = (incoming, outputs, jnp.zeros((width, experts), jnp.float32))
    final = lax.fori_loop(0, steps, loop_before, start_carry)
    outputs = final[1]
    grad_rows = summed_on_arrival(final[2].astype(jnp.bfloat16), DP, 0)
    return (outputs[None], grad_rows[None])


def solution(mesh):
    torus = Mesh(mesh.devices.reshape(mesh.shape["section"], 4, 8), ("section", "dp_0", "dp_1"))
    in_specs = (
        P(None, DP, None),
        P("section", None),
        P("section", None, None),
        P("section", DP, None, None),
        P("section", DP, None, None),
        P("section", DP, None, None),
        P("section", None, DP, None),
    )
    out_specs = (P("section", None, DP, None), P("section", DP, None))
    return jax.shard_map(
        on_device, mesh=torus, in_specs=in_specs, out_specs=out_specs, check_vma=False
    )
```

```python
import functools

import jax
import jax.numpy as jnp
from jax import lax
from jax.experimental import pallas as pl
from jax.experimental.pallas import tpu as pltpu
from jax.sharding import Mesh
from jax.sharding import PartitionSpec as P

EPSILON = 1e-06
MESH = pl.DeviceIdType.MESH
BF16 = jnp.bfloat16
F32 = jnp.float32
CAP = 7
PARTS = 8
GROUP = CAP * PARTS
TILES = GROUP // 8


def dot(a, b):
    return jnp.dot(a, b, preferred_element_type=F32)


def dot_nt(a, b):
    return lax.dot_general(a, b, (((1,), (1,)), ((), ())), preferred_element_type=F32)


def dot_tn(a, b):
    return lax.dot_general(a, b, (((0,), (0,)), ((), ())), preferred_element_type=F32)


def remote(src, dst, send_sem, recv_sem, device):
    return pltpu.make_async_remote_copy(
        src_ref=src, dst_ref=dst, send_sem=send_sem, recv_sem=recv_sem, device_id=device, device_id_type=MESH
    )


def batches_of(nx, nz):
    pairs = [[nz // 2, 0]] + [[d, nz - d] for d in range(nz // 2 - 1, 0, -1)]
    pairs = pairs[:-2] + [pairs[-2] + pairs[-1]]
    steps = sorted(range(nx), key=lambda i: (-min(i, nx - i), i))
    return [[(k, i) for k in ks for i in steps] for ks in pairs], [k for ks in pairs for k in ks], steps


def kernel(
    sizes,
    tokens_hbm,
    gain_hbm,
    router_hbm,
    routing_hbm,
    gate_hbm,
    up_hbm,
    down_hbm,
    out,
    grad,
    w_gate,
    w_up,
    w_down,
    w_router,
    gain,
    routing,
    states,
    states_before,
    normed_all,
    slope_all,
    code_all,
    match_all,
    pattern,
    pattern_t,
    spread,
    sent,
    arrived,
    hidden,
    regroup,
    regroup_t,
    whole,
    paired,
    produced,
    returned,
    combine,
    naming,
    naming_before,
    count_own,
    count_in,
    grad_own,
    grad_in,
    w_sem,
    in_sem,
    d_send,
    d_recv,
    r_send,
    r_recv,
    own_sem,
    own_send,
    side_send,
    side_recv,
    o_send,
    o_recv,
    c_send,
    c_recv,
    g_send,
    g_recv,
    go,
):
    sections, nx, nz, total_rows = sizes
    micro, stacked, part_width = out.shape
    rows, width = stacked // PARTS, part_width * PARTS
    experts = w_router.shape[0]
    topk = routing.shape[0]
    replicas = nx * nz
    slots = replicas * GROUP
    s = lax.axis_index("section")
    x = lax.axis_index("dp_0")
    z = lax.axis_index("dp_1")
    batches, k_order, i_order = batches_of(nx, nz)
    order = [step for batch in batches for step in batch]
    own = order.index((0, 0))
    starts = [0]
    for batch in batches:
        starts.append(starts[-1] + len(batch))
    own_batch = max(b for b in range(len(batches)) if starts[b] <= own)
    last = s == sections - 1
    quad_rows = nx * 8

    def ahead(j):
        k, i = order[j]
        return {"dp_0": lax.rem(x + i, nx), "dp_1": lax.rem(z + k, nz)}

    def behind(j, section):
        k, i = order[j]
        return {"section": section, "dp_0": lax.rem(x + nx - i, nx), "dp_1": lax.rem(z + nz - k, nz)}

    others = [j for j in range(replicas) if j != own]

    small = [
        pltpu.make_async_copy(routing_hbm, routing, in_sem.at[0]),
        pltpu.make_async_copy(gain_hbm, gain, in_sem.at[1]),
        pltpu.make_async_copy(router_hbm, w_router, in_sem.at[2]),
    ]
    for copy in small:
        copy.start()
    load_tokens = [
        pltpu.make_async_copy(
            tokens_hbm.at[:, :, pl.ds(p * part_width, part_width)], states.at[:, pl.ds(p * rows, rows)], in_sem.at[3 + p]
        )
        for p in range(PARTS)
    ]

    @pl.when(s == 0)
    def _():
        for copy in load_tokens:
            copy.start()

    weights = [
        pltpu.make_async_copy(gate_hbm, w_gate, w_sem.at[0]),
        pltpu.make_async_copy(up_hbm, w_up, w_sem.at[1]),
        pltpu.make_async_copy(down_hbm, w_down, w_sem.at[2]),
    ]
    for copy in weights:
        copy.start()

    barrier = pltpu.get_barrier_semaphore()
    for j in others:
        pl.semaphore_signal(barrier, inc=1, device_id=ahead(j), device_id_type=MESH)

    @pl.when(s > 0)
    def _():
        for j in range(replicas):
            pl.semaphore_signal(barrier, inc=1, device_id=behind(j, s - 1), device_id_type=MESH)

    @pl.when(s < sections - 1)
    def _():
        pl.semaphore_signal(barrier, inc=1, device_id={"section": s + 1}, device_id_type=MESH)

    e_row = lax.broadcasted_iota(jnp.int32, (experts, rows), 0)
    before = (
        lax.broadcasted_iota(jnp.int32, (rows, rows), 0) < lax.broadcasted_iota(jnp.int32, (rows, rows), 1)
    ).astype(BF16)
    row = lax.broadcasted_iota(jnp.int32, (slots, experts), 0)
    k_pos = row // (GROUP * nx)
    i_pos = (row // GROUP) % nx
    k_of = jnp.zeros_like(row)
    for p, k in enumerate(k_order):
        k_of = jnp.where(k_pos == p, k, k_of)
    i_of = jnp.zeros_like(row)
    for p, i in enumerate(i_order):
        i_of = jnp.where(i_pos == p, i, i_of)
    zz = k_of + z
    zz = jnp.where(zz >= nz, zz - nz, zz)
    xx = i_of + x
    xx = jnp.where(xx >= nx, xx - nx, xx)
    spread[...] = (lax.broadcasted_iota(jnp.int32, (slots, experts), 1) == xx * nz + zz).astype(BF16)

    g_place = lax.broadcasted_iota(jnp.int32, (slots, stacked), 0) % GROUP
    g_part = lax.broadcasted_iota(jnp.int32, (slots, stacked), 1) // rows
    pattern[...] = jnp.where(g_place // CAP == g_part, g_place % CAP, -9).astype(F32)
    t_place = lax.broadcasted_iota(jnp.int32, (stacked, slots), 1) % GROUP
    t_part = lax.broadcasted_iota(jnp.int32, (stacked, slots), 0) // rows
    pattern_t[...] = jnp.where(t_place // CAP == t_part, t_place % CAP, -9).astype(F32)

    def regrouping(shape, tall, wide):
        there = lax.broadcasted_iota(jnp.int32, shape, tall)
        here = lax.broadcasted_iota(jnp.int32, shape, wide)
        inside = here % GROUP
        same = jnp.logical_and(there // quad_rows == inside // CAP, (there % quad_rows) // 8 == here // GROUP)
        return jnp.logical_and(same, there % 8 == inside % CAP).astype(BF16)

    regroup[...] = regrouping(regroup.shape, 0, 1)
    regroup_t[...] = regrouping(regroup_t.shape, 1, 0)
    count_own[...] = jnp.zeros_like(count_own)

    def stack(block):
        return jnp.concatenate([block] * PARTS, axis=0)

    def prepare(m, _):
        hot = jnp.zeros((experts, rows), F32)
        for k in range(topk):
            hot = hot + (routing[k, pl.ds(m, 1)] == e_row).astype(F32)
        rank = dot(hot.astype(BF16), before)
        code = jnp.where(hot > 0, rank, -1.0).T
        count_own[...] = count_own[...] + jnp.sum((code >= 0).astype(F32), axis=0, keepdims=True)
        code_all[m] = code
        there = dot_nt(spread[...], stack(code.astype(BF16)))
        match_all[m] = (there == pattern[...]).astype(BF16)
        return 0

    def combining(code, mixing):
        there = dot_nt(stack(code), spread[...])
        share_there = dot_nt(stack(mixing), spread[...])
        return jnp.where(there == pattern_t[...], share_there, 0.0).astype(BF16)

    for copy in small:
        copy.wait()
    prepare(0, 0)

    @pl.when(s > 0)
    def _():
        lax.fori_loop(1, micro, prepare, 0)

    @pl.when(s == 0)
    def _():
        for copy in load_tokens:
            copy.wait()

    upward = (s < sections - 1).astype(jnp.int32)
    downward = (s > 0).astype(jnp.int32)
    pl.semaphore_wait(barrier, (replicas - 1) + replicas * upward + downward)

    count_copies = [remote(count_own, count_in.at[j], c_send, c_recv, ahead(j)) for j in others]

    def quad(q):
        return pl.ds(q * nx * GROUP, nx * GROUP)

    def span(b):
        return pl.ds(starts[b] * GROUP, (starts[b + 1] - starts[b]) * GROUP)

    def bytes_of(b, whole=True):
        count = starts[b + 1] - starts[b] - (1 if b == own_batch and not whole else 0)
        return pl.ds(starts[b] * TILES, count * TILES)

    def at(j):
        return pl.ds(j * TILES, TILES)

    def wait_sent(ref, b, sem):
        part = ref.at[bytes_of(b, False)]
        remote(part, part, sem.at[b], d_recv.at[0, b], ahead(0)).wait_send()

    def wait_back(index, b):
        part = returned.at[index, bytes_of(b)]
        remote(part, part, r_send.at[b], r_recv.at[index, b], ahead(0)).wait_recv()

    def keep(m):
        return pltpu.make_async_copy(sent.at[at(own)], arrived.at[m, at(own)], own_sem)

    def back(j, b, index, section, send_sem):
        return remote(produced.at[at(j)], returned.at[index, at(j)], send_sem, r_recv.at[index, b], behind(j, section))

    def side(m, section):
        here = {"section": section}
        return [
            remote(states.at[m], states_before.at[m], side_send.at[0, m], side_recv.at[0, m], here),
            remote(naming.at[m], naming_before.at[m], side_send.at[1, m], side_recv.at[1, m], here),
        ]

    def give(m, section):
        return remote(states.at[m], out.at[m], o_send.at[m], o_recv.at[m], {"section": section})

    def expert_ffn(m, b):
        quads = (starts[b + 1] - starts[b]) // nx
        count = quads * quad_rows
        received = arrived.at[m].reshape(slots, part_width)
        for q in range(quads):
            mine = dot(regroup[...], received[quad(starts[b] // nx + q)]).astype(BF16)
            for p in range(PARTS):
                whole[pl.ds(q * quad_rows, quad_rows), p * part_width : (p + 1) * part_width] = mine[
                    p * quad_rows : (p + 1) * quad_rows
                ]
        used = pl.ds(0, count)
        here = whole[used]
        piece = 256

        def inner(t, _):
            cols = pl.ds(pl.multiple_of(t * piece, piece), piece)
            gated = dot(here, w_gate[:, cols])
            upward = dot(here, w_up[:, cols])
            hidden[used, cols] = (gated / (1.0 + jnp.exp(-gated)) * upward).astype(BF16)
            return 0

        lax.fori_loop(0, w_gate.shape[1] // piece, inner, 0)
        now = hidden[used]

        def outer(t, _):
            cols = pl.ds(pl.multiple_of(t * 2 * part_width, 2 * part_width), 2 * part_width)
            made = dot(now, w_down[:, cols]).astype(BF16)
            for h in range(2):
                at_row = pl.multiple_of((2 * t + h) * quad_rows, quad_rows)
                for q in range(quads):
                    paired[q, pl.ds(at_row, quad_rows)] = made[
                        q * quad_rows : (q + 1) * quad_rows, h * part_width : (h + 1) * part_width
                    ]
            return 0

        lax.fori_loop(0, PARTS // 2, outer, 0)
        sending = produced.reshape(slots, part_width)
        for q in range(quads):
            sending[quad(starts[b] // nx + q)] = dot(regroup_t[...], paired[q]).astype(BF16)

    def mixed_rows(matrix, index):
        total = None
        for b in range(len(batches)):
            wait_back(index, b)
            first, past = starts[b] * GROUP, starts[b + 1] * GROUP
            part = dot(matrix[:, first:past], returned.at[index].reshape(slots, part_width)[span(b)])
            total = part if total is None else total + part
        return total

    def one(m, _):
        @pl.when(s > 0)
        def _():
            for copy in side(m, s):
                copy.wait_recv()
            combine[...] = combining(naming_before[m, 0], naming_before[m, 1])
            states[m] = (states_before[m].astype(F32) + mixed_rows(combine, m)).astype(BF16)
            give(m, s - 1).start()

        @pl.when(jnp.logical_and(s == 0, m > 0))
        def _():
            pl.semaphore_wait(go, 1)

        values = states[m].astype(F32)
        squares = jnp.sum(values * values, axis=-1, keepdims=True)
        scale = lax.rsqrt(sum(squares[p * rows : (p + 1) * rows] for p in range(PARTS)) / width + EPSILON)
        for p in range(PARTS):
            factor = gain[:, p * part_width : (p + 1) * part_width].astype(F32)
            here = slice(p * rows, (p + 1) * rows)
            normed_all[m, here] = (values[here] * scale * factor).astype(BF16)
        normed = normed_all[m]

        for b in range(len(batches)):
            @pl.when(m > 0)
            def _():
                wait_sent(sent, b, d_send)

            sent.reshape(slots, part_width)[span(b)] = dot(match_all[m, span(b)], normed).astype(BF16)
            for j in range(starts[b], starts[b + 1]):
                if j != own:
                    remote(sent.at[at(j)], arrived.at[m, at(j)], d_send.at[b], d_recv.at[m, b], ahead(j)).start()
                else:
                    keep(m).start()

        logits = sum(
            dot_nt(normed[p * rows : (p + 1) * rows], w_router[:, p * part_width : (p + 1) * part_width])
            for p in range(PARTS)
        )
        exps = jnp.exp(logits)
        probs = exps / jnp.sum(exps, axis=-1, keepdims=True)
        chosen = jnp.where(code_all[m] >= 0, probs, 0.0)
        mixing = (chosen / jnp.sum(chosen, axis=-1, keepdims=True)).astype(BF16)
        naming[m, 0] = code_all[m].astype(BF16)
        naming[m, 1] = mixing
        slope_all[m] = probs

        @pl.when(s < sections - 1)
        def _():
            for copy in side(m, s + 1):
                copy.start()

        @pl.when(jnp.logical_and(m == 0, s == 0))
        def _():
            lax.fori_loop(1, micro, prepare, 0)

        @pl.when(m == 0)
        def _():
            for copy in count_copies:
                copy.start()
            count_in[own] = count_own[...]
            for copy in weights:
                copy.wait()

        keep(m).wait()
        for b in range(len(batches)):
            part = arrived.at[m, bytes_of(b, False)]
            remote(part, part, d_send.at[b], d_recv.at[m, b], ahead(0)).wait_recv()

            expert_ffn(m, b)
            index = jnp.where(last, micro + m, m)
            to = jnp.where(last, s, s + 1)
            for j in range(starts[b], starts[b + 1]):
                if j != own:
                    back(j, b, index, to, r_send.at[b]).start()
                else:
                    @pl.when(jnp.logical_not(last))
                    def _():
                        back(j, b, m, s + 1, own_send).start()

                    @pl.when(last)
                    def _():
                        pltpu.make_async_copy(
                            produced.at[at(j)], returned.at[micro + m, at(j)], r_recv.at[micro + m, b]
                        ).start()

        @pl.when(m == micro - 1)
        def _():
            part = count_in.at[pl.ds(0, replicas - 1)]
            remote(part, part, c_send, c_recv, ahead(0)).wait()
            total = jnp.sum(count_in[...], axis=0)[0:1]
            share = experts * total / (topk * total_rows)
            for mm in range(micro):
                p = slope_all[mm]
                slope_all[mm] = p * (share - jnp.sum(p * share, axis=-1, keepdims=True))
            slope = slope_all[...].reshape(micro * rows, experts)
            high = slope.astype(BF16)
            low = (slope - high.astype(F32)).astype(BF16)
            for t in range(width // 128):
                h, c = divmod(t * 128, part_width)
                some = normed_all[:, h * rows : (h + 1) * rows, c : c + 128].reshape(micro * rows, 128)
                grad_own[t] = (dot_tn(high, some) + dot_tn(low, some)).astype(BF16)
            for j in others:
                k, i = order[j]
                where = lax.rem(x + i, nx) * nz + lax.rem(z + k, nz)
                remote(grad_own.at[where // 2], grad_in.at[j], g_send, g_recv, ahead(j)).start()
            grad_in[own] = grad_own[(x * nz + z) // 2]

        @pl.when(last)
        def _():
            combine[...] = combining(naming[m, 0], naming[m, 1])
            out[m] = (states[m].astype(F32) + mixed_rows(combine, micro + m)).astype(BF16)

        for b in range(len(batches)):
            wait_sent(produced, b, r_send)

        @pl.when(jnp.logical_not(last))
        def _():
            back(own, own_batch, m, s + 1, own_send).wait_send()

        @pl.when(jnp.logical_and(s == 1, m < micro - 1))
        def _():
            pl.semaphore_signal(go, inc=1, device_id={"section": 0}, device_id_type=MESH)

        return 0

    lax.fori_loop(0, micro, one, 0)

    part = grad_in.at[pl.ds(0, replicas - 1)]
    remote(part, part, g_send, g_recv, ahead(0)).wait()
    summed = jnp.sum(grad_in[...].astype(F32), axis=0)
    take = summed.shape[1] // 2
    grad[...] = jnp.where(lax.rem(z, 2) == 0, summed[:, :take], summed[:, take:])
    for b in range(len(batches)):
        wait_sent(sent, b, d_send)

    @pl.when(jnp.logical_not(last))
    def _():
        for m in range(micro):
            for copy in side(m, s + 1):
                copy.wait_send()
            give(m, s).wait_recv()

    @pl.when(s > 0)
    def _():
        for m in range(micro):
            give(m, s - 1).wait_send()


def on_device(sizes, tokens, norm_gain, router_weight, gate_weight, up_weight, down_weight, routing):
    sections, nx, nz, total_rows = sizes
    replicas = nx * nz
    micro, rows, width = tokens.shape
    experts = router_weight.shape[2]
    hidden = gate_weight.shape[3]
    topk = routing.shape[3]
    slots = replicas * GROUP
    part, stacked = width // PARTS, rows * PARTS
    quad = nx * 8
    most = 4 * quad
    vmem = pl.BlockSpec(memory_space=pltpu.VMEM)
    hbm = pl.BlockSpec(memory_space=pltpu.MemorySpace.HBM)
    dma = pltpu.SemaphoreType.DMA
    outputs, gradient = pl.pallas_call(
        functools.partial(kernel, sizes),
        out_shape=(
            jax.ShapeDtypeStruct((micro, stacked, part), BF16),
            jax.ShapeDtypeStruct((experts, width // replicas), F32),
        ),
        in_specs=[hbm] * 7,
        out_specs=(vmem, vmem),
        scratch_shapes=[
            pltpu.VMEM((width, hidden), BF16),
            pltpu.VMEM((width, hidden), BF16),
            pltpu.VMEM((hidden, width), BF16),
            pltpu.VMEM((experts, width), BF16),
            pltpu.VMEM((1, width), BF16),
            pltpu.VMEM((topk, micro, rows), jnp.int32),
            pltpu.VMEM((micro, stacked, part), BF16),
            pltpu.VMEM((micro, stacked, part), BF16),
            pltpu.VMEM((micro, stacked, part), BF16),
            pltpu.VMEM((micro, rows, experts), F32),
            pltpu.VMEM((micro, rows, experts), F32),
            pltpu.VMEM((micro, slots, stacked), BF16),
            pltpu.VMEM((slots, stacked), F32),
            pltpu.VMEM((stacked, slots), F32),
            pltpu.VMEM((slots, experts), BF16),
            pltpu.VMEM((slots // 8, 8, part), BF16),
            pltpu.VMEM((micro, slots // 8, 8, part), BF16),
            pltpu.VMEM((most, hidden), BF16),
            pltpu.VMEM((PARTS * quad, nx * GROUP), BF16),
            pltpu.VMEM((nx * GROUP, PARTS * quad), BF16),
            pltpu.VMEM((most, width), BF16),
            pltpu.VMEM((4, PARTS * quad, part), BF16),
            pltpu.VMEM((slots // 8, 8, part), BF16),
            pltpu.VMEM((2 * micro, slots // 8, 8, part), BF16),
            pltpu.VMEM((stacked, slots), BF16),
            pltpu.VMEM((micro, 2, rows, experts), BF16),
            pltpu.VMEM((micro, 2, rows, experts), BF16),
            pltpu.VMEM((8, experts), F32),
            pltpu.VMEM((replicas, 8, experts), F32),
            pltpu.VMEM((width // 128, experts, 128), BF16),
            pltpu.VMEM((replicas, experts, 128), BF16),
            dma((3,)),
            dma((3 + PARTS,)),
            dma((nz // 2,)),
            dma((micro, nz // 2)),
            dma((nz // 2,)),
            dma((2 * micro, nz // 2)),
            dma(()),
            dma(()),
            dma((2, micro)),
            dma((2, micro)),
            dma((micro,)),
            dma((micro,)),
            dma(()),
            dma(()),
            dma(()),
            dma(()),
            pltpu.SemaphoreType.REGULAR,
        ],
        compiler_params=pltpu.CompilerParams(
            collective_id=0, has_side_effects=True, vmem_limit_bytes=58 * 1024 * 1024
        ),
    )(tokens, norm_gain, router_weight[0].T, routing[0].transpose(2, 0, 1), gate_weight[0, 0], up_weight[0, 0], down_weight[0, 0])
    outputs = outputs.reshape(micro, PARTS, rows, part).transpose(0, 2, 1, 3).reshape(micro, rows, width)
    return outputs[None], gradient.T[None]


def solution(mesh):
    nx, nz = 4, mesh.shape["dp"] // 4
    torus = Mesh(mesh.devices.reshape(mesh.shape["section"], nx, nz), ("section", "dp_0", "dp_1"))
    dp = ("dp_0", "dp_1")

    def run(tokens, norm_gain, router_weight, gate_weight, up_weight, down_weight, routing):
        total_rows = tokens.shape[0] * tokens.shape[1]
        sizes = (mesh.shape["section"], nx, nz, total_rows)
        return jax.shard_map(
            functools.partial(on_device, sizes),
            mesh=torus,
            in_specs=(
                P(None, dp, None),
                P("section", None),
                P("section", None, None),
                P("section", dp, None, None),
                P("section", dp, None, None),
                P("section", dp, None, None),
                P("section", None, dp, None),
            ),
            out_specs=(P("section", None, dp, None), P("section", dp, None)),
            check_vma=False,
        )(tokens, norm_gain, router_weight, gate_weight, up_weight, down_weight, routing)

    return run
```

```python
import functools

import jax
import jax.numpy as jnp
from jax import lax
from jax.experimental import pallas as pl
from jax.experimental.pallas import tpu as pltpu
from jax.sharding import Mesh
from jax.sharding import PartitionSpec as P

EPSILON = 1e-06
MESH = pl.DeviceIdType.MESH
BF16 = jnp.bfloat16
F32 = jnp.float32
CAP = 7
PARTS = 8
GROUP = CAP * PARTS
TILES = GROUP // 8


def dot(a, b):
    return jnp.dot(a, b, preferred_element_type=F32)


def dot_nt(a, b):
    return lax.dot_general(a, b, (((1,), (1,)), ((), ())), preferred_element_type=F32)


def dot_tn(a, b):
    return lax.dot_general(a, b, (((0,), (0,)), ((), ())), preferred_element_type=F32)


def remote(src, dst, send_sem, recv_sem, device):
    return pltpu.make_async_remote_copy(
        src_ref=src, dst_ref=dst, send_sem=send_sem, recv_sem=recv_sem, device_id=device, device_id_type=MESH
    )


def batches_of(nx, nz):
    pairs = [[nz // 2, 0]] + [[d, nz - d] for d in range(nz // 2 - 1, 0, -1)]
    steps = sorted(range(nx), key=lambda i: (-min(i, nx - i), i))
    return [[(k, i) for k in ks for i in steps] for ks in pairs], [k for ks in pairs for k in ks], steps


def kernel(
    sizes,
    tokens_hbm,
    gain_hbm,
    router_hbm,
    routing_hbm,
    gate_hbm,
    up_hbm,
    down_hbm,
    out,
    grad,
    w_gate,
    w_up,
    w_down,
    w_router,
    gain,
    routing,
    states,
    states_before,
    normed_all,
    slope_all,
    code_all,
    match_all,
    pattern,
    pattern_t,
    spread,
    sent,
    arrived,
    hidden,
    regroup,
    regroup_t,
    whole,
    paired,
    produced,
    returned,
    combine,
    naming,
    naming_before,
    count_own,
    count_in,
    grad_own,
    grad_in,
    w_sem,
    in_sem,
    d_send,
    d_recv,
    r_send,
    r_recv,
    own_sem,
    own_send,
    side_send,
    side_recv,
    o_send,
    o_recv,
    c_send,
    c_recv,
    g_send,
    g_recv,
    go,
):
    sections, nx, nz, total_rows = sizes
    micro, rows, width = out.shape
    part_width = width // PARTS
    stacked = rows * PARTS
    experts = w_router.shape[0]
    topk = routing.shape[0]
    replicas = nx * nz
    slots = replicas * GROUP
    s = lax.axis_index("section")
    x = lax.axis_index("dp_0")
    z = lax.axis_index("dp_1")
    batches, k_order, i_order = batches_of(nx, nz)
    order = [step for batch in batches for step in batch]
    own = order.index((0, 0))
    starts = [0]
    for batch in batches:
        starts.append(starts[-1] + len(batch))
    own_batch = max(b for b in range(len(batches)) if starts[b] <= own)
    last = s == sections - 1
    quad_rows = nx * 8

    def ahead(j):
        k, i = order[j]
        return {"dp_0": lax.rem(x + i, nx), "dp_1": lax.rem(z + k, nz)}

    def behind(j, section):
        k, i = order[j]
        return {"section": section, "dp_0": lax.rem(x + nx - i, nx), "dp_1": lax.rem(z + nz - k, nz)}

    others = [j for j in range(replicas) if j != own]

    small = [
        pltpu.make_async_copy(routing_hbm, routing, in_sem.at[0]),
        pltpu.make_async_copy(gain_hbm, gain, in_sem.at[1]),
        pltpu.make_async_copy(router_hbm, w_router, in_sem.at[2]),
    ]
    for copy in small:
        copy.start()
    load_tokens = [
        pltpu.make_async_copy(
            tokens_hbm.at[:, :, pl.ds(p * part_width, part_width)], states.at[:, pl.ds(p * rows, rows)], in_sem.at[3 + p]
        )
        for p in range(PARTS)
    ]

    @pl.when(s == 0)
    def _():
        for copy in load_tokens:
            copy.start()

    weights = [
        pltpu.make_async_copy(gate_hbm, w_gate, w_sem.at[0]),
        pltpu.make_async_copy(up_hbm, w_up, w_sem.at[1]),
        pltpu.make_async_copy(down_hbm, w_down, w_sem.at[2]),
    ]
    for copy in weights:
        copy.start()

    barrier = pltpu.get_barrier_semaphore()
    for j in others:
        pl.semaphore_signal(barrier, inc=1, device_id=ahead(j), device_id_type=MESH)

    @pl.when(s > 0)
    def _():
        for j in range(replicas):
            pl.semaphore_signal(barrier, inc=1, device_id=behind(j, s - 1), device_id_type=MESH)

    @pl.when(s < sections - 1)
    def _():
        pl.semaphore_signal(barrier, inc=1, device_id={"section": s + 1}, device_id_type=MESH)

    e_row = lax.broadcasted_iota(jnp.int32, (experts, rows), 0)
    before = (
        lax.broadcasted_iota(jnp.int32, (rows, rows), 0) < lax.broadcasted_iota(jnp.int32, (rows, rows), 1)
    ).astype(BF16)
    row = lax.broadcasted_iota(jnp.int32, (replicas, experts), 0)
    k_pos = row // nx
    i_pos = row % nx
    k_of = jnp.zeros_like(row)
    for p, k in enumerate(k_order):
        k_of = jnp.where(k_pos == p, k, k_of)
    i_of = jnp.zeros_like(row)
    for p, i in enumerate(i_order):
        i_of = jnp.where(i_pos == p, i, i_of)
    zz = k_of + z
    zz = jnp.where(zz >= nz, zz - nz, zz)
    xx = i_of + x
    xx = jnp.where(xx >= nx, xx - nx, xx)
    named = (lax.broadcasted_iota(jnp.int32, (replicas, experts), 1) == xx * nz + zz).astype(F32)
    for j in range(replicas):
        spread[pl.ds(j * GROUP, GROUP)] = jnp.broadcast_to(named[j : j + 1], (GROUP, experts)).astype(BF16)

    g_place = lax.broadcasted_iota(jnp.int32, (GROUP, stacked), 0)
    g_part = lax.broadcasted_iota(jnp.int32, (GROUP, stacked), 1) // rows
    pattern[...] = jnp.where(g_place // CAP == g_part, g_place % CAP, -9).astype(F32)
    t_place = lax.broadcasted_iota(jnp.int32, (PARTS, slots), 1) % GROUP
    t_part = lax.broadcasted_iota(jnp.int32, (PARTS, slots), 0)
    pattern_t[...] = jnp.where(t_place // CAP == t_part, t_place % CAP, -9).astype(F32)

    def regrouping(shape, tall, wide):
        there = lax.broadcasted_iota(jnp.int32, shape, tall)
        here = lax.broadcasted_iota(jnp.int32, shape, wide)
        inside = here % GROUP
        same = jnp.logical_and(there // quad_rows == inside // CAP, (there % quad_rows) // 8 == here // GROUP)
        return jnp.logical_and(same, there % 8 == inside % CAP).astype(BF16)

    count_own[...] = jnp.zeros_like(count_own)

    def stack(block):
        return jnp.concatenate([block] * PARTS, axis=0)

    def prepare(m, _):
        hot = jnp.zeros((experts, rows), F32)
        for k in range(topk):
            hot = hot + (routing[k, pl.ds(m, 1)] == e_row).astype(F32)
        rank = dot(hot.astype(BF16), before)
        code = jnp.where(hot > 0, rank, -1.0).T
        count_own[...] = count_own[...] + jnp.sum((code >= 0).astype(F32), axis=0, keepdims=True)
        code_all[m] = code
        there = dot_nt(spread[...], stack(code.astype(BF16)))
        for j in range(replicas):
            group = slice(j * GROUP, (j + 1) * GROUP)
            match_all[m, group] = (there[group] == pattern[...]).astype(BF16)
        return 0

    def combining(code, mixing):
        there = dot_nt(stack(code), spread[...])
        share_there = dot_nt(stack(mixing), spread[...])
        for p in range(PARTS):
            here = slice(p * rows, (p + 1) * rows)
            fits = there[here] == pattern_t[p : p + 1]
            combine[here] = jnp.where(fits, share_there[here], 0.0).astype(BF16)

    for copy in small:
        copy.wait()
    prepare(0, 0)

    def prepare_rest():
        regroup[...] = regrouping(regroup.shape, 0, 1)
        regroup_t[...] = regrouping(regroup_t.shape, 1, 0)
        lax.fori_loop(1, micro, prepare, 0)

    @pl.when(s > 0)
    def _():
        prepare_rest()

    @pl.when(s == 0)
    def _():
        for copy in load_tokens:
            copy.wait()

    upward = (s < sections - 1).astype(jnp.int32)
    downward = (s > 0).astype(jnp.int32)
    pl.semaphore_wait(barrier, (replicas - 1) + replicas * upward + downward)

    count_copies = [remote(count_own, count_in.at[j], c_send, c_recv, ahead(j)) for j in others]

    def quad(q):
        return pl.ds(q * nx * GROUP, nx * GROUP)

    def span(b):
        return pl.ds(starts[b] * GROUP, (starts[b + 1] - starts[b]) * GROUP)

    def bytes_of(b, whole=True):
        count = starts[b + 1] - starts[b] - (1 if b == own_batch and not whole else 0)
        return pl.ds(starts[b] * TILES, count * TILES)

    def at(j):
        return pl.ds(j * TILES, TILES)

    def wait_sent(ref, b, sem):
        part = ref.at[bytes_of(b, False)]
        remote(part, part, sem.at[b], d_recv.at[0, b], ahead(0)).wait_send()

    def wait_back(index, b):
        part = returned.at[index, bytes_of(b)]
        remote(part, part, r_send.at[b], r_recv.at[index, b], ahead(0)).wait_recv()

    def keep(m):
        return pltpu.make_async_copy(sent.at[at(own)], arrived.at[m, at(own)], own_sem)

    def back(j, b, index, section, send_sem):
        return remote(produced.at[at(j)], returned.at[index, at(j)], send_sem, r_recv.at[index, b], behind(j, section))

    def side(m, section):
        here = {"section": section}
        return [
            remote(states.at[m], states_before.at[m], side_send.at[0, m], side_recv.at[0, m], here),
            remote(naming.at[m], naming_before.at[m], side_send.at[1, m], side_recv.at[1, m], here),
        ]

    def give(m, section):
        return [
            remote(
                states.at[m, pl.ds(p * rows, rows)],
                out.at[m, :, pl.ds(p * part_width, part_width)],
                o_send.at[m],
                o_recv.at[m],
                {"section": section},
            )
            for p in range(PARTS)
        ]

    def expert_ffn(m, b):
        quads = (starts[b + 1] - starts[b]) // nx
        count = quads * quad_rows
        received = arrived.at[m].reshape(slots, part_width)
        for q in range(quads):
            mine = dot(regroup[...], received[quad(starts[b] // nx + q)]).astype(BF16)
            for p in range(PARTS):
                whole[pl.ds(q * quad_rows, quad_rows), p * part_width : (p + 1) * part_width] = mine[
                    p * quad_rows : (p + 1) * quad_rows
                ]
        used = pl.ds(0, count)
        here = whole[used]
        piece = 256

        def inner(t, _):
            cols = pl.ds(pl.multiple_of(t * piece, piece), piece)
            gated = dot(here, w_gate[:, cols])
            upward = dot(here, w_up[:, cols])
            hidden[used, cols] = (gated / (1.0 + jnp.exp(-gated)) * upward).astype(BF16)
            return 0

        lax.fori_loop(0, w_gate.shape[1] // piece, inner, 0, unroll=True)
        now = hidden[used]

        def outer(t, _):
            cols = pl.ds(pl.multiple_of(t * 2 * part_width, 2 * part_width), 2 * part_width)
            made = dot(now, w_down[:, cols]).astype(BF16)
            for h in range(2):
                at_row = pl.multiple_of((2 * t + h) * quad_rows, quad_rows)
                for q in range(quads):
                    paired[q, pl.ds(at_row, quad_rows)] = made[
                        q * quad_rows : (q + 1) * quad_rows, h * part_width : (h + 1) * part_width
                    ]
            return 0

        lax.fori_loop(0, PARTS // 2, outer, 0, unroll=True)
        sending = produced.reshape(slots, part_width)
        for q in range(quads):
            sending[quad(starts[b] // nx + q)] = dot(regroup_t[...], paired[q]).astype(BF16)

    def mixed_rows(matrix, index):
        total = None
        for b in range(len(batches)):
            wait_back(index, b)
            first, past = starts[b] * GROUP, starts[b + 1] * GROUP
            part = dot(matrix[:, first:past], returned.at[index].reshape(slots, part_width)[span(b)])
            total = part if total is None else total + part
        return total

    def one(m, _):
        @pl.when(s > 0)
        def _():
            for copy in side(m, s):
                copy.wait_recv()
            combining(naming_before[m, 0], naming_before[m, 1])
            states[m] = (states_before[m].astype(F32) + mixed_rows(combine, m)).astype(BF16)

        @pl.when(jnp.logical_and(s == 0, m > 0))
        def _():
            pl.semaphore_wait(go, 1)

        values = states[m].astype(F32)
        squares = jnp.sum(values * values, axis=-1, keepdims=True)
        scale = lax.rsqrt(sum(squares[p * rows : (p + 1) * rows] for p in range(PARTS)) / width + EPSILON)
        for p in range(PARTS):
            factor = gain[:, p * part_width : (p + 1) * part_width].astype(F32)
            here = slice(p * rows, (p + 1) * rows)
            normed_all[m, here] = (values[here] * scale * factor).astype(BF16)
        normed = normed_all[m]

        for b in range(len(batches)):
            @pl.when(m > 0)
            def _():
                wait_sent(sent, b, d_send)

            sent.reshape(slots, part_width)[span(b)] = dot(match_all[m, span(b)], normed).astype(BF16)
            for j in range(starts[b], starts[b + 1]):
                if j != own:
                    remote(sent.at[at(j)], arrived.at[m, at(j)], d_send.at[b], d_recv.at[m, b], ahead(j)).start()
                else:
                    keep(m).start()

        logits = sum(
            dot_nt(normed[p * rows : (p + 1) * rows], w_router[:, p * part_width : (p + 1) * part_width])
            for p in range(PARTS)
        )
        exps = jnp.exp(logits)
        probs = exps / jnp.sum(exps, axis=-1, keepdims=True)
        chosen = jnp.where(code_all[m] >= 0, probs, 0.0)
        mixing = (chosen / jnp.sum(chosen, axis=-1, keepdims=True)).astype(BF16)
        naming[m, 0] = code_all[m].astype(BF16)
        naming[m, 1] = mixing
        slope_all[m] = probs

        @pl.when(s < sections - 1)
        def _():
            for copy in side(m, s + 1):
                copy.start()

        @pl.when(s > 0)
        def _():
            for copy in give(m, s - 1):
                copy.start()

        @pl.when(jnp.logical_and(m == 0, s == 0))
        def _():
            prepare_rest()

        @pl.when(m == 0)
        def _():
            for copy in count_copies:
                copy.start()
            count_in[own] = count_own[...]
            for copy in weights:
                copy.wait()

        keep(m).wait()
        for b in range(len(batches)):
            part = arrived.at[m, bytes_of(b, False)]
            remote(part, part, d_send.at[b], d_recv.at[m, b], ahead(0)).wait_recv()

            expert_ffn(m, b)
            index = jnp.where(last, micro + m, m)
            to = jnp.where(last, s, s + 1)
            for j in range(starts[b], starts[b + 1]):
                if j != own:
                    back(j, b, index, to, r_send.at[b]).start()
                else:
                    @pl.when(jnp.logical_not(last))
                    def _():
                        back(j, b, m, s + 1, own_send).start()

                    @pl.when(last)
                    def _():
                        pltpu.make_async_copy(
                            produced.at[at(j)], returned.at[micro + m, at(j)], r_recv.at[micro + m, b]
                        ).start()

        @pl.when(m == micro - 1)
        def _():
            part = count_in.at[pl.ds(0, replicas - 1)]
            remote(part, part, c_send, c_recv, ahead(0)).wait()
            total = jnp.sum(count_in[...], axis=0)[0:1]
            share = experts * total / (topk * total_rows)
            for mm in range(micro):
                p = slope_all[mm]
                slope_all[mm] = p * (share - jnp.sum(p * share, axis=-1, keepdims=True))
            slope = slope_all[...].reshape(micro * rows, experts)
            high = slope.astype(BF16)
            low = (slope - high.astype(F32)).astype(BF16)
            for t in range(width // 128):
                h, c = divmod(t * 128, part_width)
                some = normed_all[:, h * rows : (h + 1) * rows, c : c + 128].reshape(micro * rows, 128)
                grad_own[t] = (dot_tn(high, some) + dot_tn(low, some)).astype(BF16)
            for j in others:
                k, i = order[j]
                where = lax.rem(x + i, nx) * nz + lax.rem(z + k, nz)
                remote(grad_own.at[where // 2], grad_in.at[j], g_send, g_recv, ahead(j)).start()
            grad_in[own] = grad_own[(x * nz + z) // 2]

        @pl.when(last)
        def _():
            combining(naming[m, 0], naming[m, 1])
            result = (states[m].astype(F32) + mixed_rows(combine, micro + m)).astype(BF16)
            for p in range(PARTS):
                out[m, :, p * part_width : (p + 1) * part_width] = result[p * rows : (p + 1) * rows]

        for b in range(len(batches)):
            wait_sent(produced, b, r_send)

        @pl.when(jnp.logical_not(last))
        def _():
            back(own, own_batch, m, s + 1, own_send).wait_send()

        @pl.when(jnp.logical_and(s == 1, m < micro - 1))
        def _():
            pl.semaphore_signal(go, inc=1, device_id={"section": 0}, device_id_type=MESH)

        return 0

    lax.fori_loop(0, micro, one, 0)

    part = grad_in.at[pl.ds(0, replicas - 1)]
    remote(part, part, g_send, g_recv, ahead(0)).wait()
    summed = jnp.sum(grad_in[...].astype(F32), axis=0)
    take = summed.shape[1] // 2
    grad[...] = jnp.where(lax.rem(z, 2) == 0, summed[:, :take], summed[:, take:])
    for b in range(len(batches)):
        wait_sent(sent, b, d_send)

    @pl.when(jnp.logical_not(last))
    def _():
        for m in range(micro):
            for copy in side(m, s + 1):
                copy.wait_send()
            remote(out.at[m], out.at[m], o_send.at[m], o_recv.at[m], {"section": s}).wait_recv()

    @pl.when(s > 0)
    def _():
        for m in range(micro):
            remote(states.at[m], states.at[m], o_send.at[m], o_recv.at[m], {"section": s}).wait_send()


def on_device(sizes, tokens, norm_gain, router_weight, gate_weight, up_weight, down_weight, routing):
    sections, nx, nz, total_rows = sizes
    replicas = nx * nz
    micro, rows, width = tokens.shape
    experts = router_weight.shape[2]
    hidden = gate_weight.shape[3]
    topk = routing.shape[3]
    slots = replicas * GROUP
    part, stacked = width // PARTS, rows * PARTS
    quad = nx * 8
    most = 4 * quad
    vmem = pl.BlockSpec(memory_space=pltpu.VMEM)
    hbm = pl.BlockSpec(memory_space=pltpu.MemorySpace.HBM)
    dma = pltpu.SemaphoreType.DMA
    outputs, gradient = pl.pallas_call(
        functools.partial(kernel, sizes),
        out_shape=(
            jax.ShapeDtypeStruct((micro, rows, width), BF16),
            jax.ShapeDtypeStruct((experts, width // replicas), F32),
        ),
        in_specs=[hbm] * 7,
        out_specs=(vmem, vmem),
        scratch_shapes=[
            pltpu.VMEM((width, hidden), BF16),
            pltpu.VMEM((width, hidden), BF16),
            pltpu.VMEM((hidden, width), BF16),
            pltpu.VMEM((experts, width), BF16),
            pltpu.VMEM((1, width), BF16),
            pltpu.VMEM((topk, micro, rows), jnp.int32),
            pltpu.VMEM((micro, stacked, part), BF16),
            pltpu.VMEM((micro, stacked, part), BF16),
            pltpu.VMEM((micro, stacked, part), BF16),
            pltpu.VMEM((micro, rows, experts), F32),
            pltpu.VMEM((micro, rows, experts), F32),
            pltpu.VMEM((micro, slots, stacked), BF16),
            pltpu.VMEM((GROUP, stacked), F32),
            pltpu.VMEM((PARTS, slots), F32),
            pltpu.VMEM((slots, experts), BF16),
            pltpu.VMEM((slots // 8, 8, part), BF16),
            pltpu.VMEM((micro, slots // 8, 8, part), BF16),
            pltpu.VMEM((most, hidden), BF16),
            pltpu.VMEM((PARTS * quad, nx * GROUP), BF16),
            pltpu.VMEM((nx * GROUP, PARTS * quad), BF16),
            pltpu.VMEM((most, width), BF16),
            pltpu.VMEM((4, PARTS * quad, part), BF16),
            pltpu.VMEM((slots // 8, 8, part), BF16),
            pltpu.VMEM((2 * micro, slots // 8, 8, part), BF16),
            pltpu.VMEM((stacked, slots), BF16),
            pltpu.VMEM((micro, 2, rows, experts), BF16),
            pltpu.VMEM((micro, 2, rows, experts), BF16),
            pltpu.VMEM((8, experts), F32),
            pltpu.VMEM((replicas, 8, experts), F32),
            pltpu.VMEM((width // 128, experts, 128), BF16),
            pltpu.VMEM((replicas, experts, 128), BF16),
            dma((3,)),
            dma((3 + PARTS,)),
            dma((nz // 2,)),
            dma((micro, nz // 2)),
            dma((nz // 2,)),
            dma((2 * micro, nz // 2)),
            dma(()),
            dma(()),
            dma((2, micro)),
            dma((2, micro)),
            dma((micro,)),
            dma((micro,)),
            dma(()),
            dma(()),
            dma(()),
            dma(()),
            pltpu.SemaphoreType.REGULAR,
        ],
        compiler_params=pltpu.CompilerParams(
            collective_id=0, has_side_effects=True, vmem_limit_bytes=58 * 1024 * 1024
        ),
    )(tokens, norm_gain, router_weight[0].T, routing[0].transpose(2, 0, 1), gate_weight[0, 0], up_weight[0, 0], down_weight[0, 0])
    return outputs[None], gradient.T[None]


def solution(mesh):
    nx, nz = 4, mesh.shape["dp"] // 4
    torus = Mesh(mesh.devices.reshape(mesh.shape["section"], nx, nz), ("section", "dp_0", "dp_1"))
    dp = ("dp_0", "dp_1")

    def run(tokens, norm_gain, router_weight, gate_weight, up_weight, down_weight, routing):
        total_rows = tokens.shape[0] * tokens.shape[1]
        sizes = (mesh.shape["section"], nx, nz, total_rows)
        return jax.shard_map(
            functools.partial(on_device, sizes),
            mesh=torus,
            in_specs=(
                P(None, dp, None),
                P("section", None),
                P("section", None, None),
                P("section", dp, None, None),
                P("section", dp, None, None),
                P("section", dp, None, None),
                P("section", None, dp, None),
            ),
            out_specs=(P("section", None, dp, None), P("section", dp, None)),
            check_vma=False,
        )(tokens, norm_gain, router_weight, gate_weight, up_weight, down_weight, routing)

    return run
```

```python
import functools

import jax
import jax.numpy as jnp
from jax import lax
from jax.experimental import pallas as pl
from jax.experimental.pallas import tpu as pltpu
from jax.sharding import Mesh
from jax.sharding import PartitionSpec as P

EPSILON = 1e-06
MESH = pl.DeviceIdType.MESH
BF16 = jnp.bfloat16
F32 = jnp.float32
CAP = 7
PARTS = 8
GROUP = CAP * PARTS
TILES = GROUP // 8


def dot(a, b):
    return jnp.dot(a, b, preferred_element_type=F32)


def dot_nt(a, b):
    return lax.dot_general(a, b, (((1,), (1,)), ((), ())), preferred_element_type=F32)


def dot_tn(a, b):
    return lax.dot_general(a, b, (((0,), (0,)), ((), ())), preferred_element_type=F32)


def remote(src, dst, send_sem, recv_sem, device):
    return pltpu.make_async_remote_copy(
        src_ref=src, dst_ref=dst, send_sem=send_sem, recv_sem=recv_sem, device_id=device, device_id_type=MESH
    )


def batches_of(nx, nz):
    pairs = [[nz // 2, 0]] + [[d, nz - d] for d in range(nz // 2 - 1, 0, -1)]
    steps = sorted(range(nx), key=lambda i: (-min(i, nx - i), i))
    return [[(k, i) for k in ks for i in steps] for ks in pairs], [k for ks in pairs for k in ks], steps


def kernel(
    sizes,
    tokens_hbm,
    gain_hbm,
    router_hbm,
    routing_hbm,
    gate_hbm,
    up_hbm,
    down_hbm,
    out,
    grad,
    w_gate,
    w_up,
    w_down,
    w_router,
    gain,
    routing,
    states,
    states_before,
    normed_all,
    slope_all,
    code_all,
    match_all,
    pattern,
    pattern_t,
    spread,
    sent,
    arrived,
    hidden,
    regroup,
    regroup_t,
    whole,
    paired,
    produced,
    returned,
    combine,
    naming,
    naming_before,
    count_own,
    count_in,
    grad_own,
    grad_in,
    w_sem,
    in_sem,
    d_send,
    d_recv,
    r_send,
    r_recv,
    own_sem,
    own_send,
    side_send,
    side_recv,
    o_send,
    o_recv,
    c_send,
    c_recv,
    g_send,
    g_recv,
    go,
    quiet,
):
    sections, nx, nz, total_rows = sizes
    micro, rows, width = out.shape
    part_width = width // PARTS
    stacked = rows * PARTS
    experts = w_router.shape[0]
    topk = routing.shape[0]
    replicas = nx * nz
    slots = replicas * GROUP
    s = lax.axis_index("section")
    x = lax.axis_index("dp_0")
    z = lax.axis_index("dp_1")
    batches, k_order, i_order = batches_of(nx, nz)
    order = [step for batch in batches for step in batch]
    own = order.index((0, 0))
    starts = [0]
    for batch in batches:
        starts.append(starts[-1] + len(batch))
    own_batch = max(b for b in range(len(batches)) if starts[b] <= own)
    last = s == sections - 1
    quad_rows = nx * 8

    def ahead(j):
        k, i = order[j]
        return {"dp_0": lax.rem(x + i, nx), "dp_1": lax.rem(z + k, nz)}

    def behind(j, section):
        k, i = order[j]
        return {"section": section, "dp_0": lax.rem(x + nx - i, nx), "dp_1": lax.rem(z + nz - k, nz)}

    others = [j for j in range(replicas) if j != own]

    small = [
        pltpu.make_async_copy(routing_hbm, routing, in_sem.at[0]),
        pltpu.make_async_copy(gain_hbm, gain, in_sem.at[1]),
        pltpu.make_async_copy(router_hbm, w_router, in_sem.at[2]),
    ]
    for copy in small:
        copy.start()
    load_tokens = [
        pltpu.make_async_copy(
            tokens_hbm.at[:, :, pl.ds(p * part_width, part_width)], states.at[:, pl.ds(p * rows, rows)], in_sem.at[3 + p]
        )
        for p in range(PARTS)
    ]

    @pl.when(s == 0)
    def _():
        for copy in load_tokens:
            copy.start()

    weights = [
        pltpu.make_async_copy(gate_hbm, w_gate, w_sem.at[0]),
        pltpu.make_async_copy(up_hbm, w_up, w_sem.at[1]),
        pltpu.make_async_copy(down_hbm, w_down, w_sem.at[2]),
    ]
    for copy in weights:
        copy.start()

    barrier = pltpu.get_barrier_semaphore()
    for j in others:
        pl.semaphore_signal(barrier, inc=1, device_id=ahead(j), device_id_type=MESH)

    @pl.when(s > 0)
    def _():
        for j in range(replicas):
            pl.semaphore_signal(barrier, inc=1, device_id=behind(j, s - 1), device_id_type=MESH)

    @pl.when(s < sections - 1)
    def _():
        pl.semaphore_signal(barrier, inc=1, device_id={"section": s + 1}, device_id_type=MESH)

    e_row = lax.broadcasted_iota(jnp.int32, (experts, rows), 0)
    before = (
        lax.broadcasted_iota(jnp.int32, (rows, rows), 0) < lax.broadcasted_iota(jnp.int32, (rows, rows), 1)
    ).astype(BF16)
    row = lax.broadcasted_iota(jnp.int32, (replicas, experts), 0)
    k_pos = row // nx
    i_pos = row % nx
    k_of = jnp.zeros_like(row)
    for p, k in enumerate(k_order):
        k_of = jnp.where(k_pos == p, k, k_of)
    i_of = jnp.zeros_like(row)
    for p, i in enumerate(i_order):
        i_of = jnp.where(i_pos == p, i, i_of)
    zz = k_of + z
    zz = jnp.where(zz >= nz, zz - nz, zz)
    xx = i_of + x
    xx = jnp.where(xx >= nx, xx - nx, xx)
    named = (lax.broadcasted_iota(jnp.int32, (replicas, experts), 1) == xx * nz + zz).astype(F32)
    for j in range(replicas):
        spread[pl.ds(j * GROUP, GROUP)] = jnp.broadcast_to(named[j : j + 1], (GROUP, experts)).astype(BF16)

    g_place = lax.broadcasted_iota(jnp.int32, (GROUP, stacked), 0)
    g_part = lax.broadcasted_iota(jnp.int32, (GROUP, stacked), 1) // rows
    pattern[...] = jnp.where(g_place // CAP == g_part, g_place % CAP, -9).astype(F32)
    t_place = lax.broadcasted_iota(jnp.int32, (PARTS, slots), 1) % GROUP
    t_part = lax.broadcasted_iota(jnp.int32, (PARTS, slots), 0)
    pattern_t[...] = jnp.where(t_place // CAP == t_part, t_place % CAP, -9).astype(F32)

    def regrouping(shape, tall, wide):
        there = lax.broadcasted_iota(jnp.int32, shape, tall)
        here = lax.broadcasted_iota(jnp.int32, shape, wide)
        inside = here % GROUP
        same = jnp.logical_and(there // quad_rows == inside // CAP, (there % quad_rows) // 8 == here // GROUP)
        return jnp.logical_and(same, there % 8 == inside % CAP).astype(BF16)

    count_own[...] = jnp.zeros_like(count_own)

    def stack(block):
        return jnp.concatenate([block] * PARTS, axis=0)

    def prepare(m, _):
        hot = jnp.zeros((experts, rows), F32)
        for k in range(topk):
            hot = hot + (routing[k, pl.ds(m, 1)] == e_row).astype(F32)
        rank = dot(hot.astype(BF16), before)
        code = jnp.where(hot > 0, rank, -1.0).T
        count_own[...] = count_own[...] + jnp.sum((code >= 0).astype(F32), axis=0, keepdims=True)
        code_all[m] = code
        there = dot_nt(spread[...], stack(code.astype(BF16)))
        for j in range(replicas):
            group = slice(j * GROUP, (j + 1) * GROUP)
            match_all[m, group] = (there[group] == pattern[...]).astype(BF16)
        return 0

    def combining(code, mixing):
        there = dot_nt(stack(code), spread[...])
        share_there = dot_nt(stack(mixing), spread[...])
        for p in range(PARTS):
            here = slice(p * rows, (p + 1) * rows)
            fits = there[here] == pattern_t[p : p + 1]
            combine[here] = jnp.where(fits, share_there[here], 0.0).astype(BF16)

    for copy in small:
        copy.wait()
    prepare(0, 0)

    def prepare_rest():
        regroup[...] = regrouping(regroup.shape, 0, 1)
        regroup_t[...] = regrouping(regroup_t.shape, 1, 0)
        lax.fori_loop(1, micro, prepare, 0)

    @pl.when(s > 0)
    def _():
        prepare_rest()

    @pl.when(s == 0)
    def _():
        for copy in load_tokens:
            copy.wait()

    upward = (s < sections - 1).astype(jnp.int32)
    downward = (s > 0).astype(jnp.int32)
    pl.semaphore_wait(barrier, (replicas - 1) + replicas * upward + downward)

    count_copies = [remote(count_own, count_in.at[j], c_send, c_recv, ahead(j)) for j in others]

    def quad(q):
        return pl.ds(q * nx * GROUP, nx * GROUP)

    def span(b):
        return pl.ds(starts[b] * GROUP, (starts[b + 1] - starts[b]) * GROUP)

    def bytes_of(b, whole=True):
        count = starts[b + 1] - starts[b] - (1 if b == own_batch and not whole else 0)
        return pl.ds(starts[b] * TILES, count * TILES)

    def at(j):
        return pl.ds(j * TILES, TILES)

    def wait_sent(ref, b, sem):
        part = ref.at[bytes_of(b, False)]
        remote(part, part, sem.at[b], d_recv.at[0, b], ahead(0)).wait_send()

    def wait_back(index, b):
        part = returned.at[index, bytes_of(b)]
        remote(part, part, r_send.at[b], r_recv.at[index, b], ahead(0)).wait_recv()

    def keep(m):
        return pltpu.make_async_copy(sent.at[at(own)], arrived.at[m, at(own)], own_sem)

    def back(j, b, index, section, send_sem):
        return remote(produced.at[at(j)], returned.at[index, at(j)], send_sem, r_recv.at[index, b], behind(j, section))

    def side(m, section):
        here = {"section": section}
        return [
            remote(states.at[m], states_before.at[m], side_send.at[0, m], side_recv.at[0, m], here),
            remote(naming.at[m], naming_before.at[m], side_send.at[1, m], side_recv.at[1, m], here),
        ]

    def give(m, section):
        return [
            remote(
                states.at[m, pl.ds(p * rows, rows)],
                out.at[m, :, pl.ds(p * part_width, part_width)],
                o_send.at[m],
                o_recv.at[m],
                {"section": section},
            )
            for p in range(PARTS)
        ]

    def expert_ffn(m, b):
        quads = (starts[b + 1] - starts[b]) // nx
        count = quads * quad_rows
        received = arrived.at[m].reshape(slots, part_width)
        for q in range(quads):
            mine = dot(regroup[...], received[quad(starts[b] // nx + q)]).astype(BF16)
            for p in range(PARTS):
                whole[pl.ds(q * quad_rows, quad_rows), p * part_width : (p + 1) * part_width] = mine[
                    p * quad_rows : (p + 1) * quad_rows
                ]
        used = pl.ds(0, count)
        here = whole[used]
        piece = 256

        def inner(t, _):
            cols = pl.ds(pl.multiple_of(t * piece, piece), piece)
            gated = dot(here, w_gate[:, cols])
            upward = dot(here, w_up[:, cols])
            hidden[used, cols] = (gated / (1.0 + jnp.exp(-gated)) * upward).astype(BF16)
            return 0

        lax.fori_loop(0, w_gate.shape[1] // piece, inner, 0, unroll=True)
        now = hidden[used]

        def outer(t, _):
            cols = pl.ds(pl.multiple_of(t * 2 * part_width, 2 * part_width), 2 * part_width)
            made = dot(now, w_down[:, cols]).astype(BF16)
            for h in range(2):
                at_row = pl.multiple_of((2 * t + h) * quad_rows, quad_rows)
                for q in range(quads):
                    paired[q, pl.ds(at_row, quad_rows)] = made[
                        q * quad_rows : (q + 1) * quad_rows, h * part_width : (h + 1) * part_width
                    ]
            return 0

        lax.fori_loop(0, PARTS // 2, outer, 0, unroll=True)
        sending = produced.reshape(slots, part_width)
        for q in range(quads):
            sending[quad(starts[b] // nx + q)] = dot(regroup_t[...], paired[q]).astype(BF16)

    def mixed_rows(matrix, index):
        total = None
        for b in range(len(batches)):
            wait_back(index, b)
            first, past = starts[b] * GROUP, starts[b + 1] * GROUP
            part = dot(matrix[:, first:past], returned.at[index].reshape(slots, part_width)[span(b)])
            total = part if total is None else total + part
        return total

    def gradient_out():
        part = count_in.at[pl.ds(0, replicas - 1)]
        remote(part, part, c_send, c_recv, ahead(0)).wait()
        total = jnp.sum(count_in[...], axis=0)[0:1]
        share = experts * total / (topk * total_rows)
        for mm in range(micro):
            p = slope_all[mm]
            slope_all[mm] = p * (share - jnp.sum(p * share, axis=-1, keepdims=True))
        slope = slope_all[...].reshape(micro * rows, experts)
        high = slope.astype(BF16)
        low = (slope - high.astype(F32)).astype(BF16)
        for t in range(width // 128):
            h, c = divmod(t * 128, part_width)
            some = normed_all[:, h * rows : (h + 1) * rows, c : c + 128].reshape(micro * rows, 128)
            grad_own[t] = (dot_tn(high, some) + dot_tn(low, some)).astype(BF16)
        for j in others:
            k, i = order[j]
            where = lax.rem(x + i, nx) * nz + lax.rem(z + k, nz)
            remote(grad_own.at[where // 2], grad_in.at[j], g_send, g_recv, ahead(j)).start()
        grad_in[own] = grad_own[(x * nz + z) // 2]

    def one(m, _):
        @pl.when(s > 0)
        def _():
            for copy in side(m, s):
                copy.wait_recv()
            combining(naming_before[m, 0], naming_before[m, 1])
            states[m] = (states_before[m].astype(F32) + mixed_rows(combine, m)).astype(BF16)

        @pl.when(jnp.logical_and(s == 0, m > 0))
        def _():
            pl.semaphore_wait(go, 1)

        values = states[m].astype(F32)
        squares = jnp.sum(values * values, axis=-1, keepdims=True)
        scale = lax.rsqrt(sum(squares[p * rows : (p + 1) * rows] for p in range(PARTS)) / width + EPSILON)
        for p in range(PARTS):
            factor = gain[:, p * part_width : (p + 1) * part_width].astype(F32)
            here = slice(p * rows, (p + 1) * rows)
            normed_all[m, here] = (values[here] * scale * factor).astype(BF16)
        normed = normed_all[m]

        for b in range(len(batches)):
            @pl.when(m > 0)
            def _():
                wait_sent(sent, b, d_send)

            sent.reshape(slots, part_width)[span(b)] = dot(match_all[m, span(b)], normed).astype(BF16)
            for j in range(starts[b], starts[b + 1]):
                if j != own:
                    remote(sent.at[at(j)], arrived.at[m, at(j)], d_send.at[b], d_recv.at[m, b], ahead(j)).start()
                else:
                    keep(m).start()

        logits = sum(
            dot_nt(normed[p * rows : (p + 1) * rows], w_router[:, p * part_width : (p + 1) * part_width])
            for p in range(PARTS)
        )
        exps = jnp.exp(logits)
        probs = exps / jnp.sum(exps, axis=-1, keepdims=True)
        chosen = jnp.where(code_all[m] >= 0, probs, 0.0)
        mixing = (chosen / jnp.sum(chosen, axis=-1, keepdims=True)).astype(BF16)
        naming[m, 0] = code_all[m].astype(BF16)
        naming[m, 1] = mixing
        slope_all[m] = probs

        @pl.when(s < sections - 1)
        def _():
            for copy in side(m, s + 1):
                copy.start()

        @pl.when(s > 0)
        def _():
            for copy in give(m, s - 1):
                copy.start()

        @pl.when(jnp.logical_and(m == 0, s == 0))
        def _():
            prepare_rest()

        @pl.when(m == 0)
        def _():
            for copy in count_copies:
                copy.start()
            count_in[own] = count_own[...]
            for copy in weights:
                copy.wait()

        keep(m).wait()
        for b in range(len(batches)):
            part = arrived.at[m, bytes_of(b, False)]
            remote(part, part, d_send.at[b], d_recv.at[m, b], ahead(0)).wait_recv()

            expert_ffn(m, b)
            index = jnp.where(last, micro + m, m)
            to = jnp.where(last, s, s + 1)
            for j in range(starts[b], starts[b + 1]):
                if j != own:
                    back(j, b, index, to, r_send.at[b]).start()
                else:
                    @pl.when(jnp.logical_not(last))
                    def _():
                        back(j, b, m, s + 1, own_send).start()

                    @pl.when(last)
                    def _():
                        pltpu.make_async_copy(
                            produced.at[at(j)], returned.at[micro + m, at(j)], r_recv.at[micro + m, b]
                        ).start()

        @pl.when(jnp.logical_and(m == micro - 1, s >= sections - 2))
        def _():
            gradient_out()

        @pl.when(last)
        def _():
            combining(naming[m, 0], naming[m, 1])
            result = (states[m].astype(F32) + mixed_rows(combine, micro + m)).astype(BF16)
            for p in range(PARTS):
                out[m, :, p * part_width : (p + 1) * part_width] = result[p * rows : (p + 1) * rows]

        for b in range(len(batches)):
            wait_sent(produced, b, r_send)

        @pl.when(jnp.logical_not(last))
        def _():
            back(own, own_batch, m, s + 1, own_send).wait_send()

        @pl.when(jnp.logical_and(s == 1, m < micro - 1))
        def _():
            pl.semaphore_signal(go, inc=1, device_id={"section": 0}, device_id_type=MESH)

        @pl.when(jnp.logical_and(m == micro - 1, jnp.logical_and(s < sections - 2, lax.rem(s, 2) == 1)))
        def _():
            pl.semaphore_signal(quiet, inc=1, device_id={"section": s - 1}, device_id_type=MESH)

        return 0

    lax.fori_loop(0, micro, one, 0)

    @pl.when(jnp.logical_not(last))
    def _():
        for m in range(micro):
            for copy in side(m, s + 1):
                copy.wait_send()
            remote(out.at[m], out.at[m], o_send.at[m], o_recv.at[m], {"section": s}).wait_recv()

    @pl.when(s > 0)
    def _():
        for m in range(micro):
            remote(states.at[m], states.at[m], o_send.at[m], o_recv.at[m], {"section": s}).wait_send()

    @pl.when(jnp.logical_and(s < sections - 2, lax.rem(s, 2) == 0))
    def _():
        pl.semaphore_wait(quiet, 1)

    @pl.when(s < sections - 2)
    def _():
        gradient_out()

    part = grad_in.at[pl.ds(0, replicas - 1)]
    remote(part, part, g_send, g_recv, ahead(0)).wait()
    summed = jnp.sum(grad_in[...].astype(F32), axis=0)
    take = summed.shape[1] // 2
    grad[...] = jnp.where(lax.rem(z, 2) == 0, summed[:, :take], summed[:, take:])
    for b in range(len(batches)):
        wait_sent(sent, b, d_send)


def on_device(sizes, tokens, norm_gain, router_weight, gate_weight, up_weight, down_weight, routing):
    sections, nx, nz, total_rows = sizes
    replicas = nx * nz
    micro, rows, width = tokens.shape
    experts = router_weight.shape[2]
    hidden = gate_weight.shape[3]
    topk = routing.shape[3]
    slots = replicas * GROUP
    part, stacked = width // PARTS, rows * PARTS
    quad = nx * 8
    most = 4 * quad
    vmem = pl.BlockSpec(memory_space=pltpu.VMEM)
    hbm = pl.BlockSpec(memory_space=pltpu.MemorySpace.HBM)
    dma = pltpu.SemaphoreType.DMA
    outputs, gradient = pl.pallas_call(
        functools.partial(kernel, sizes),
        out_shape=(
            jax.ShapeDtypeStruct((micro, rows, width), BF16),
            jax.ShapeDtypeStruct((experts, width // replicas), F32),
        ),
        in_specs=[hbm] * 7,
        out_specs=(vmem, vmem),
        scratch_shapes=[
            pltpu.VMEM((width, hidden), BF16),
            pltpu.VMEM((width, hidden), BF16),
            pltpu.VMEM((hidden, width), BF16),
            pltpu.VMEM((experts, width), BF16),
            pltpu.VMEM((1, width), BF16),
            pltpu.VMEM((topk, micro, rows), jnp.int32),
            pltpu.VMEM((micro, stacked, part), BF16),
            pltpu.VMEM((micro, stacked, part), BF16),
            pltpu.VMEM((micro, stacked, part), BF16),
            pltpu.VMEM((micro, rows, experts), F32),
            pltpu.VMEM((micro, rows, experts), F32),
            pltpu.VMEM((micro, slots, stacked), BF16),
            pltpu.VMEM((GROUP, stacked), F32),
            pltpu.VMEM((PARTS, slots), F32),
            pltpu.VMEM((slots, experts), BF16),
            pltpu.VMEM((slots // 8, 8, part), BF16),
            pltpu.VMEM((micro, slots // 8, 8, part), BF16),
            pltpu.VMEM((most, hidden), BF16),
            pltpu.VMEM((PARTS * quad, nx * GROUP), BF16),
            pltpu.VMEM((nx * GROUP, PARTS * quad), BF16),
            pltpu.VMEM((most, width), BF16),
            pltpu.VMEM((4, PARTS * quad, part), BF16),
            pltpu.VMEM((slots // 8, 8, part), BF16),
            pltpu.VMEM((2 * micro, slots // 8, 8, part), BF16),
            pltpu.VMEM((stacked, slots), BF16),
            pltpu.VMEM((micro, 2, rows, experts), BF16),
            pltpu.VMEM((micro, 2, rows, experts), BF16),
            pltpu.VMEM((8, experts), F32),
            pltpu.VMEM((replicas, 8, experts), F32),
            pltpu.VMEM((width // 128, experts, 128), BF16),
            pltpu.VMEM((replicas, experts, 128), BF16),
            dma((3,)),
            dma((3 + PARTS,)),
            dma((nz // 2,)),
            dma((micro, nz // 2)),
            dma((nz // 2,)),
            dma((2 * micro, nz // 2)),
            dma(()),
            dma(()),
            dma((2, micro)),
            dma((2, micro)),
            dma((micro,)),
            dma((micro,)),
            dma(()),
            dma(()),
            dma(()),
            dma(()),
            pltpu.SemaphoreType.REGULAR,
            pltpu.SemaphoreType.REGULAR,
        ],
        compiler_params=pltpu.CompilerParams(
            collective_id=0, has_side_effects=True, vmem_limit_bytes=58 * 1024 * 1024
        ),
    )(tokens, norm_gain, router_weight[0].T, routing[0].transpose(2, 0, 1), gate_weight[0, 0], up_weight[0, 0], down_weight[0, 0])
    return outputs[None], gradient.T[None]


def solution(mesh):
    nx, nz = 4, mesh.shape["dp"] // 4
    torus = Mesh(mesh.devices.reshape(mesh.shape["section"], nx, nz), ("section", "dp_0", "dp_1"))
    dp = ("dp_0", "dp_1")

    def run(tokens, norm_gain, router_weight, gate_weight, up_weight, down_weight, routing):
        total_rows = tokens.shape[0] * tokens.shape[1]
        sizes = (mesh.shape["section"], nx, nz, total_rows)
        return jax.shard_map(
            functools.partial(on_device, sizes),
            mesh=torus,
            in_specs=(
                P(None, dp, None),
                P("section", None),
                P("section", None, None),
                P("section", dp, None, None),
                P("section", dp, None, None),
                P("section", dp, None, None),
                P("section", None, dp, None),
            ),
            out_specs=(P("section", None, dp, None), P("section", dp, None)),
            check_vma=False,
        )(tokens, norm_gain, router_weight, gate_weight, up_weight, down_weight, routing)

    return run
```
